32 devices in a mesh: row: 4 (over y, x), col: 8 (over z, core).
Axes of the slice: x: 2, y: 2, z: 4, core: 2. Of those that a mesh axis runs over, the one named last changes fastest.
Arguments:
- layer_input: float32 [2048, 1088], P('col', 'row'), may hold values from -6 to 6
- output_grad: float32 [2048, 1088], P('col', 'row'), may hold values from -6 to 6
- w_qkv: float32 [1088, 6144], P('row', 'col'), as said below
- w_out: float32 [2048, 1088], P('col', 'row'), as said below
- w_up: float32 [1088, 4352], P('row', 'col'), may hold values from -0.1875 to 0.1875
- w_down: float32 [4352, 1088], P('col', 'row'), may hold values from -0.09375 to 0.09375
- layernorm_params: float32 [4, 1088], P(None, 'row')
- state_qkv: float32 [2, 1088, 6144], P(None, 'row', 'col'), as said below
- state_out: float32 [2, 2048, 1088], P(None, 'col', 'row'), as said below
- state_up: float32 [2, 1088, 4352], P(None, 'row', 'col'), as said below
- state_down: float32 [2, 4352, 1088], P(None, 'col', 'row'), as said below
- state_norms: float32 [2, 4, 1088], P(None, None, 'row'), as said below
- segment_ids: int32 [4, 512], P('row'), may hold values from 0 to 2, as said below
Outputs:
- block_output: float32 [2048, 1088], P('col', 'row')
- layer_input_grad: float32 [2048, 1088], P('col', 'row')
- grad_qkv: float32 [1088, 6144], P('row', 'col')
- grad_out: float32 [2048, 1088], P('col', 'row')
- grad_up: float32 [1088, 4352], P('row', 'col')
- grad_down: float32 [4352, 1088], P('col', 'row')
- norm_params_grad: float32 [4, 1088], P(None, 'row')
- new_qkv: float32 [1088, 6144], P('row', 'col')
- new_out: float32 [2048, 1088], P('col', 'row')
- new_up: float32 [1088, 4352], P('row', 'col')
- new_down: float32 [4352, 1088], P('col', 'row')
- new_norms: float32 [4, 1088], P(None, 'row')
- next_state_qkv: float32 [2, 1088, 6144], P(None, 'row', 'col')
- next_state_out: float32 [2, 2048, 1088], P(None, 'col', 'row')
- next_state_up: float32 [2, 1088, 4352], P(None, 'row', 'col')
- next_state_down: float32 [2, 4352, 1088], P(None, 'col', 'row')
- next_state_norms: float32 [2, 4, 1088], P(None, None, 'row')
The draws below stay inside these ranges and needn't reach their ends.
Inputs may be any that keep to these rules, and one draw needn't show every extreme that they name: `segment_ids`: within each sequence the ids never fall; each sequence holds exactly three documents, numbered 0, 1, 2, the first two of 64 or more tokens. `w_qkv`: columns of heads 17 and above are zero. `w_out`: rows of heads 17 and above are zero. `state_qkv`: both moments are zero in the columns of heads 17 and above; second moments are positive elsewhere. `state_out`: both moments are zero in the rows of heads 17 and above; second moments are positive elsewhere. `state_up`: second moments are positive. `state_down`: second moments are positive. `state_norms`: second moments are positive.
All inputs are finite; a program needn't handle non-finite values.
Results may differ from the reference program's by a relative error of at most 0.011.
Values may be sent and summed in bfloat16 or wider, within the bound.
No kernel may reach another device: no remote copies, remote signals or barrier semaphores. Data moves between devices by JAX's collectives and lax.ppermute only.
A program may use at most 128 MiB of HBM per device.

```python
import jax
import jax.numpy as jnp
from jax import lax

MODEL_WIDTH = 1088
HS = 64
HR = 17
HP = 32
FF = 4352
SEQ = 512
SEQS = 4
TOKENS = 2048


def live_heads(count, width):
    return (jnp.arange(count) // width < HR).astype(jnp.float32)


def moment_pair(key, shape, factor):
    grad_scale = factor * TOKENS ** 0.5
    first_branch = jax.random.normal(jax.random.fold_in(key, 1), shape, jnp.float32) * (0.15 * grad_scale)
    spread = jax.random.uniform(jax.random.fold_in(key, 2), shape, jnp.float32, minval=-1.0, maxval=1.0)
    second_branch = jnp.exp(spread) * (0.05 * grad_scale * grad_scale)
    return jnp.stack([first_branch, second_branch])


def draw_w_qkv(key, part):
    base = jax.random.normal(jax.random.fold_in(key, 11), (MODEL_WIDTH, 3 * HP * HS), jnp.float32)
    return base * MODEL_WIDTH ** (-0.5) * live_heads(3 * HP * HS, 3 * HS)[None, :]


def draw_w_out(key, part):
    base = jax.random.normal(jax.random.fold_in(key, 12), (HP * HS, MODEL_WIDTH), jnp.float32)
    return base * (8.0 / (HR * HS)) ** 0.5 * live_heads(HP * HS, HS)[:, None]


def draw_layernorm_params(key, part):
    gains = 1.0 + jax.random.uniform(jax.random.fold_in(key, 31), (2, MODEL_WIDTH), jnp.float32, minval=-0.3, maxval=0.3)
    biases = 0.3 * jax.random.normal(jax.random.fold_in(key, 32), (2, MODEL_WIDTH), jnp.float32)
    return jnp.stack([gains[0], biases[0], gains[1], biases[1]])


def draw_state_qkv(key, part):
    pair = moment_pair(jax.random.fold_in(key, 21), (MODEL_WIDTH, 3 * HP * HS), 1.0)
    return pair * live_heads(3 * HP * HS, 3 * HS)[None, None, :]


def draw_state_out(key, part):
    pair = moment_pair(jax.random.fold_in(key, 22), (HP * HS, MODEL_WIDTH), 0.12)
    return pair * live_heads(HP * HS, HS)[None, :, None]


def draw_state_up(key, part):
    return moment_pair(jax.random.fold_in(key, 23), (MODEL_WIDTH, FF), 0.33)


def draw_state_down(key, part):
    return moment_pair(jax.random.fold_in(key, 24), (FF, MODEL_WIDTH), 0.6)


def draw_state_norms(key, part):
    return moment_pair(jax.random.fold_in(key, 25), (4, MODEL_WIDTH), 1.0)


def draw_segment_ids(key, part):
    first_branch = jax.random.randint(jax.random.fold_in(key, 41), (SEQS, 1), SEQ // 8, SEQ // 2)
    second_branch = first_branch + jax.random.randint(jax.random.fold_in(key, 42), (SEQS, 1), SEQ // 8, SEQ // 2)
    place = jnp.arange(SEQ, dtype=jnp.int32)[None, :]
    return (place >= first_branch).astype(jnp.int32) + (place >= second_branch).astype(jnp.int32)


def levels(stream_key, extent, cuts, least, high):
    factor_of, own = 1.0, jax.random.fold_in(stream_key, 6)
    for dim, shards_of in cuts:
        heights = jnp.exp(jax.random.uniform(jax.random.fold_in(own, dim), (shards_of,), jnp.float32, least / len(cuts), high / len(cuts)))
        factor_of = factor_of * jnp.repeat(heights, extent[dim] // shards_of).reshape([-1 if axis == dim else 1 for axis in range(len(extent))])
    return factor_of


def centred(rng, extent, scale, bound, split=(), held_as=jnp.bfloat16):
    drawn = scale * jax.random.normal(rng, extent, jnp.float32)
    if split:
        drawn = drawn * levels(rng, extent, split, -0.22, 0.18)
    return jnp.clip(drawn, -bound, bound).astype(held_as)


def setup_inputs(seed: int = 0) -> dict:
    splits = jax.random.split(jax.random.key(seed), 14)
    layer_input = centred(splits[0], (TOKENS, MODEL_WIDTH), 1.0, 6.0, ((0, 8), (1, 4)), jnp.float32)
    output_grad = centred(splits[1], (TOKENS, MODEL_WIDTH), 1.0, 6.0, ((0, 8), (1, 4)), jnp.float32)
    w_qkv = draw_w_qkv(jax.random.fold_in(splits[13], 71), 0)
    w_out = draw_w_out(jax.random.fold_in(splits[13], 71), 0)
    w_up = centred(splits[4], (MODEL_WIDTH, FF), MODEL_WIDTH ** -0.5, 0.1875, ((0, 4), (1, 8)), jnp.float32)
    w_down = centred(splits[5], (FF, MODEL_WIDTH), FF ** -0.5, 0.09375, ((0, 8), (1, 4)), jnp.float32)
    layernorm_params = draw_layernorm_params(jax.random.fold_in(splits[13], 71), 0)
    state_qkv = draw_state_qkv(jax.random.fold_in(splits[13], 71), 0)
    state_out = draw_state_out(jax.random.fold_in(splits[13], 71), 0)
    state_up = draw_state_up(jax.random.fold_in(splits[13], 71), 0)
    state_down = draw_state_down(jax.random.fold_in(splits[13], 71), 0)
    state_norms = draw_state_norms(jax.random.fold_in(splits[13], 71), 0)
    segment_ids = draw_segment_ids(jax.random.fold_in(splits[13], 71), 0)
    return dict(layer_input=layer_input, output_grad=output_grad, w_qkv=w_qkv, w_out=w_out, w_up=w_up, w_down=w_down, layernorm_params=layernorm_params, state_qkv=state_qkv, state_out=state_out, state_up=state_up, state_down=state_down, state_norms=state_norms, segment_ids=segment_ids)


EPS_NORM = 1e-05
NEG_FILL = -1e+30
BETA_ONE = 0.9
BETA_TWO = 0.95
RATE = 0.01
DECAY = 0.1
STEP_COUNT = 3
ADAM_EPS = 1e-08

def layernorm_forward(x, norm_gain, shift_bias):
    row_mean = lax.optimization_barrier(jnp.mean(x, axis=1, keepdims=True))
    mean_removed = x - row_mean
    var = lax.optimization_barrier(jnp.mean(mean_removed * mean_removed, axis=1, keepdims=True))
    inverse_deviation = lax.rsqrt(var + EPS_NORM)
    normalized_rows = mean_removed * inverse_deviation
    return (normalized_rows, inverse_deviation, (normalized_rows * norm_gain + shift_bias).astype(jnp.bfloat16))

def layernorm_backward(incoming_grad, normalized_rows, inverse_deviation, norm_gain):
    normalized_grad = incoming_grad * norm_gain
    first_branch = lax.optimization_barrier(jnp.mean(normalized_grad, axis=1, keepdims=True))
    second_branch = lax.optimization_barrier(jnp.mean(normalized_grad * normalized_rows, axis=1, keepdims=True))
    return inverse_deviation * (normalized_grad - first_branch - normalized_rows * second_branch)

def activation(value):
    return jax.nn.gelu(value, approximate=True)

def slope(value, incoming_grad):
    return jax.vjp(activation, value)[1](incoming_grad)[0]

def masked_scores(query, keys, segment):
    scores = jnp.einsum('qhd,khd->hqk', query.astype(jnp.float32), keys.astype(jnp.float32)) * HS ** (-0.5)
    place = jnp.arange(segment.shape[0])
    allowed = (place[None, :] <= place[:, None]) & (segment[None, :] == segment[:, None])
    return jnp.where(allowed[None], scores, NEG_FILL)

def attend(item):
    block, segment = item
    query, keys, values = (block[:, :, 0], block[:, :, 1], block[:, :, 2])
    scores = masked_scores(query, keys, segment)
    top = lax.optimization_barrier(jnp.max(scores, axis=-1))
    lse = top + jnp.log(lax.optimization_barrier(jnp.sum(jnp.exp(scores - top[..., None]), axis=-1)))
    probs = jnp.exp(scores - lse[..., None]).astype(jnp.bfloat16)
    result = jnp.einsum('hqk,khd->qhd', probs.astype(jnp.float32), values.astype(jnp.float32))
    return (result.astype(jnp.bfloat16), lse)

def attend_back(item):
    block, segment, lse, incoming_grad = item
    query, keys, values = (block[:, :, 0], block[:, :, 1], block[:, :, 2])
    probs = jnp.exp(masked_scores(query, keys, segment) - lse[..., None])
    probs_low = probs.astype(jnp.bfloat16).astype(jnp.float32)
    upper = incoming_grad.astype(jnp.float32)
    dvalues = jnp.einsum('hqk,qhd->khd', probs_low, upper)
    dprobs = jnp.einsum('qhd,khd->hqk', upper, values.astype(jnp.float32))
    delta = lax.optimization_barrier(jnp.sum(probs * dprobs, axis=-1, keepdims=True))
    dscores = (probs * (dprobs - delta)).astype(jnp.bfloat16).astype(jnp.float32)
    dquery = jnp.einsum('hqk,khd->qhd', dscores, keys.astype(jnp.float32)) * HS ** (-0.5)
    dkeys = jnp.einsum('hqk,qhd->khd', dscores, query.astype(jnp.float32)) * HS ** (-0.5)
    return jnp.stack([dquery, dkeys, dvalues], axis=2).astype(jnp.bfloat16)

def adamw(param, grad, state, decay):
    first_branch = BETA_ONE * state[0] + (1.0 - BETA_ONE) * grad
    second_branch = BETA_TWO * state[1] + (1.0 - BETA_TWO) * grad * grad
    first_hat = first_branch / (1.0 - BETA_ONE ** STEP_COUNT)
    second_hat = second_branch / (1.0 - BETA_TWO ** STEP_COUNT)
    updated = param - RATE * (first_hat / (jnp.sqrt(second_hat) + ADAM_EPS) + decay * param)
    return (updated, jnp.stack([first_branch, second_branch]))

def reference(layer_input, output_grad, w_qkv, w_out, w_up, w_down, layernorm_params, state_qkv, state_out, state_up, state_down, state_norms, segment_ids):
    low = jnp.bfloat16
    wq, wo, wu, wd = (w_qkv.astype(low), w_out.astype(low), w_up.astype(low), w_down.astype(low))
    normalized_rows1, inverse_deviation1, attention_input = layernorm_forward(layer_input, layernorm_params[0], layernorm_params[1])
    qkv = jnp.dot(attention_input, wq, preferred_element_type=jnp.float32).astype(low)
    blocks = qkv.reshape(SEQS, SEQ, HP, 3, HS)
    attended, lse = lax.map(attend, (blocks, segment_ids))
    attended = attended.reshape(TOKENS, HP * HS)
    middle_stream = layer_input + jnp.dot(attended, wo, preferred_element_type=jnp.float32)
    normalized_rows2, inverse_deviation2, feedforward_input = layernorm_forward(middle_stream, layernorm_params[2], layernorm_params[3])
    pre = jnp.dot(feedforward_input, wu, preferred_element_type=jnp.float32)
    hidden = activation(pre).astype(low)
    block_output = middle_stream + jnp.dot(hidden, wd, preferred_element_type=jnp.float32)
    out_low = output_grad.astype(low)
    grad_down = jnp.dot(hidden.T, out_low, preferred_element_type=jnp.float32)
    hidden_grad = jnp.dot(out_low, wd.T, preferred_element_type=jnp.float32)
    pre_grad = slope(pre, hidden_grad).astype(low)
    grad_up = jnp.dot(feedforward_input.T, pre_grad, preferred_element_type=jnp.float32)
    feedforward_input_grad = jnp.dot(pre_grad, wu.T, preferred_element_type=jnp.float32)
    middle_stream_grad = output_grad + layernorm_backward(feedforward_input_grad, normalized_rows2, inverse_deviation2, layernorm_params[2])
    middle_low = middle_stream_grad.astype(low)
    grad_out = jnp.dot(attended.T, middle_low, preferred_element_type=jnp.float32)
    attended_grad = jnp.dot(middle_low, wo.T, preferred_element_type=jnp.float32).astype(low)
    incoming_grad = attended_grad.reshape(SEQS, SEQ, HP, HS)
    qkv_grad = lax.map(attend_back, (blocks, segment_ids, lse, incoming_grad)).reshape(TOKENS, 3 * HP * HS)
    grad_qkv = jnp.dot(attention_input.T, qkv_grad, preferred_element_type=jnp.float32)
    attention_input_grad = jnp.dot(qkv_grad, wq.T, preferred_element_type=jnp.float32)
    layer_input_grad = middle_stream_grad + layernorm_backward(attention_input_grad, normalized_rows1, inverse_deviation1, layernorm_params[0])
    norm_params_grad = jnp.stack([lax.optimization_barrier(jnp.sum(attention_input_grad * normalized_rows1, axis=0)), lax.optimization_barrier(jnp.sum(attention_input_grad, axis=0)), lax.optimization_barrier(jnp.sum(feedforward_input_grad * normalized_rows2, axis=0)), lax.optimization_barrier(jnp.sum(feedforward_input_grad, axis=0))])
    new_qkv, next_state_qkv = adamw(w_qkv, grad_qkv, state_qkv, DECAY)
    new_out, next_state_out = adamw(w_out, grad_out, state_out, DECAY)
    new_up, next_state_up = adamw(w_up, grad_up, state_up, DECAY)
    new_down, next_state_down = adamw(w_down, grad_down, state_down, DECAY)
    new_norms, next_state_norms = adamw(layernorm_params, norm_params_grad, state_norms, 0.0)
    return (block_output, layer_input_grad, grad_qkv, grad_out, grad_up, grad_down, norm_params_grad, new_qkv, new_out, new_up, new_down, new_norms, next_state_qkv, next_state_out, next_state_up, next_state_down, next_state_norms)
```

```python
import functools

import jax
import jax.numpy as jnp
from jax import lax
from jax.sharding import PartitionSpec as P

HS = 64
EPS_NORM = 1e-05
NEG_FILL = -1e30
BETA_ONE = 0.9
BETA_TWO = 0.95
RATE = 0.01
DECAY = 0.1
STEP_COUNT = 3
ADAM_EPS = 1e-08

LOW = jnp.bfloat16
F32 = jnp.float32


def dot(left, right, dims):
    return lax.dot_general(left, right, (dims, ((), ())), preferred_element_type=F32)


def select_xor(pieces, shift):
    count, bit = len(pieces), 1
    while bit < count:
        flag = (shift & bit) != 0
        pieces = [jnp.where(flag, pieces[i ^ bit], pieces[i]) for i in range(count)]
        bit *= 2
    return pieces


class Grid:
    def __init__(self, nrow, ncol):
        self.nrow, self.ncol, self.nz = nrow, ncol, ncol // 2
        self.row = lax.axis_index("row")
        self.col = lax.axis_index("col")
        self.lin = self.row * ncol + self.col

    def over_row(self, x, k):
        return lax.ppermute(x, "row", [(r, r ^ k) for r in range(self.nrow)])

    def over_chip(self, x, k):
        return lax.ppermute(x, "col", [(c, c ^ (2 * k)) for c in range(self.ncol)])

    def over_core(self, x):
        return lax.ppermute(x, "col", [(c, c ^ 1) for c in range(self.ncol)])

    def gather_row(self, x, axis):
        return jnp.concatenate(
            [x] + [self.over_row(x, k) for k in range(1, self.nrow)], axis=axis
        )

    def reduce_row(self, pieces):
        got = [self.over_row(pieces[k].astype(LOW), k) for k in range(1, self.nrow)]
        return sum([g.astype(F32) for g in got], pieces[0])

    def gather_col(self, x):
        own = jnp.concatenate([x] + [self.over_chip(x, k) for k in range(1, self.nz)], axis=0)
        return jnp.concatenate([own, self.over_core(own)], axis=0)

    def reduce_col(self, own, other):
        total = own + self.over_core(other.astype(LOW)).astype(F32)
        pieces = jnp.split(total, self.nz, axis=0)
        got = [self.over_chip(pieces[k].astype(LOW), k) for k in range(1, self.nz)]
        return sum([g.astype(F32) for g in got], pieces[0])

    def to_tokens(self, pieces):
        sent = select_xor(pieces, self.row)
        got = []
        for m in range(self.nrow):
            pairs = [
                (r * self.ncol + c, c * self.nrow + (r ^ m))
                for r in range(self.nrow)
                for c in range(self.ncol)
            ]
            got.append(lax.ppermute(sent[m], ("row", "col"), pairs))
        return select_xor(got, (self.lin % self.nrow) ^ self.row)

    def to_widths(self, pieces):
        sent = select_xor(pieces, (self.lin % self.nrow) ^ self.row)
        got = []
        for m in range(self.nrow):
            pairs = [
                (c * self.nrow + (r ^ m), r * self.ncol + c)
                for r in range(self.nrow)
                for c in range(self.ncol)
            ]
            got.append(lax.ppermute(sent[m], ("row", "col"), pairs))
        return select_xor(got, self.row)


def activation(value):
    return jax.nn.gelu(value, approximate=True)


def slope(value, incoming_grad):
    return jax.vjp(activation, value)[1](incoming_grad)[0]


def norm_forward(x, gain, bias):
    removed = x - jnp.mean(x, axis=1, keepdims=True)
    inverse = lax.rsqrt(jnp.mean(removed * removed, axis=1, keepdims=True) + EPS_NORM)
    hat = removed * inverse
    return hat, inverse, (hat * gain + bias).astype(LOW)


def norm_backward(incoming, hat, inverse, gain):
    scaled = incoming * gain
    first = jnp.mean(scaled, axis=1, keepdims=True)
    second = jnp.mean(scaled * hat, axis=1, keepdims=True)
    return inverse * (scaled - first - hat * second)


def masked_scores(query, keys, allowed):
    scores = jnp.einsum("qhd,khd->hqk", query, keys, preferred_element_type=F32) * HS ** (-0.5)
    return jnp.where(allowed[None], scores, NEG_FILL)


def attend(query, keys, values, allowed):
    scores = masked_scores(query, keys, allowed)
    top = jnp.max(scores, axis=-1)
    lse = top + jnp.log(jnp.sum(jnp.exp(scores - top[..., None]), axis=-1))
    probs = jnp.exp(scores - lse[..., None]).astype(LOW)
    result = jnp.einsum("hqk,khd->qhd", probs, values, preferred_element_type=F32)
    return result.astype(LOW), lse


def attend_back(query, keys, values, allowed, lse, incoming):
    probs = jnp.exp(masked_scores(query, keys, allowed) - lse[..., None])
    dvalues = jnp.einsum("hqk,qhd->khd", probs.astype(LOW), incoming, preferred_element_type=F32)
    dprobs = jnp.einsum("qhd,khd->hqk", incoming, values, preferred_element_type=F32)
    delta = jnp.sum(probs * dprobs, axis=-1, keepdims=True)
    dscores = (probs * (dprobs - delta)).astype(LOW)
    dquery = jnp.einsum("hqk,khd->qhd", dscores, keys, preferred_element_type=F32) * HS ** (-0.5)
    dkeys = jnp.einsum("hqk,qhd->khd", dscores, query, preferred_element_type=F32) * HS ** (-0.5)
    return jnp.stack([dquery, dkeys, dvalues], axis=2).astype(LOW)


def adamw(param, grad, state, decay):
    first = BETA_ONE * state[0] + (1.0 - BETA_ONE) * grad
    second = BETA_TWO * state[1] + (1.0 - BETA_TWO) * grad * grad
    first_hat = first / (1.0 - BETA_ONE**STEP_COUNT)
    second_hat = second / (1.0 - BETA_TWO**STEP_COUNT)
    updated = param - RATE * (first_hat / (jnp.sqrt(second_hat) + ADAM_EPS) + decay * param)
    return updated, jnp.stack([first, second])


def shards(
    nrow,
    ncol,
    layer_input,
    output_grad,
    w_qkv,
    w_out,
    w_up,
    w_down,
    layernorm_params,
    state_qkv,
    state_out,
    state_up,
    state_down,
    state_norms,
    segment_ids,
):
    grid = Grid(nrow, ncol)
    width = layer_input.shape[1]
    own_tokens = layer_input.shape[0] // nrow
    row_tokens = own_tokens * ncol

    with jax.named_scope("to_tokens"):
        high = lax.reduce_precision(layernorm_params, 8, 7)
        params_low = jnp.concatenate([high, layernorm_params - high]).astype(LOW)
        streams = jnp.stack([layer_input.astype(LOW), output_grad.astype(LOW)])
        pieces = [
            jnp.concatenate([streams[0, part], streams[1, part], params_low])
            for part in (slice(p * own_tokens, (p + 1) * own_tokens) for p in range(nrow))
        ]
        mine = jnp.concatenate(grid.to_tokens(pieces), axis=1)
        x = mine[:own_tokens].astype(F32)
        out_low = mine[own_tokens : 2 * own_tokens]
        params = mine[2 * own_tokens :].astype(F32)
        params = params[:4] + params[4:]
        gain1, bias1, gain2, bias2 = (params[i : i + 1] for i in range(4))

    with jax.named_scope("weights"):
        wq = grid.gather_row(w_qkv.astype(LOW), 0)
        wo = grid.gather_row(w_out.astype(LOW), 1)
        wd = grid.gather_row(w_down.astype(LOW), 1)
        wu = grid.gather_row(w_up.astype(LOW), 0)

    half = grid.nz * own_tokens
    with jax.named_scope("mask"):
        chip, core = grid.col // 2, grid.col % 2
        spot = jnp.arange(row_tokens)
        sequence = spot // segment_ids.shape[1]
        marks = sequence * (1 + jnp.max(segment_ids)) + segment_ids.reshape(-1)

        def reorder(values):
            values = values.reshape(grid.nz, 2, own_tokens)
            chips = select_xor([values[z] for z in range(grid.nz)], chip)
            cores = select_xor([jnp.stack([v[h] for v in chips]) for h in range(2)], core)
            return jnp.concatenate(cores).reshape(-1)

        place, mark = reorder(spot), reorder(marks)
        allowed = (place[None, :] <= place[:, None]) & (mark[None, :] == mark[:, None])

    with jax.named_scope("norm1"):
        hat1, inverse1, a1_own = norm_forward(x, gain1, bias1)
    with jax.named_scope("gather_a1"):
        a1 = grid.gather_col(a1_own)
    with jax.named_scope("qkv"):
        qkv = dot(a1, wq, ((1,), (0,))).astype(LOW).reshape(row_tokens, -1, 3, HS)
        query, keys, values = qkv[:, :, 0], qkv[:, :, 1], qkv[:, :, 2]
    with jax.named_scope("attend"):
        attended, lse = attend(query, keys, values, allowed)
        attended = attended.reshape(row_tokens, -1)
    with jax.named_scope("reduce_attn"):
        attn_sum = grid.reduce_col(
            dot(attended[:half], wo, ((1,), (0,))), dot(attended[half:], wo, ((1,), (0,)))
        )
    with jax.named_scope("norm2"):
        middle = x + attn_sum
        hat2, inverse2, a2_own = norm_forward(middle, gain2, bias2)
    with jax.named_scope("gather_out"):
        out_full = grid.gather_col(out_low)
    with jax.named_scope("gather_a2"):
        a2 = grid.gather_col(a2_own)
    with jax.named_scope("hidden_grad"):
        hidden_grad = dot(out_full, wd, ((1,), (1,)))
    with jax.named_scope("up"):
        pre = dot(a2, wu, ((1,), (0,)))
        hidden = activation(pre).astype(LOW)
        pre_grad = slope(pre, hidden_grad).astype(LOW)
    with jax.named_scope("reduce_da2"):
        da2 = grid.reduce_col(
            dot(pre_grad[:half], wu, ((1,), (1,))), dot(pre_grad[half:], wu, ((1,), (1,)))
        )
    with jax.named_scope("norm2_back"):
        back2 = norm_backward(da2, hat2, inverse2, gain2)
        middle_low_own = (out_low.astype(F32) + back2).astype(LOW)
    with jax.named_scope("gather_mid"):
        middle_low = grid.gather_col(middle_low_own)
    with jax.named_scope("attended_grad"):
        incoming = dot(middle_low, wo, ((1,), (1,))).astype(LOW).reshape(row_tokens, -1, HS)
    with jax.named_scope("attend_back"):
        qkv_grad = attend_back(query, keys, values, allowed, lse, incoming).reshape(row_tokens, -1)
    with jax.named_scope("reduce_da1"):
        da1 = grid.reduce_col(
            dot(qkv_grad[:half], wq, ((1,), (1,))), dot(qkv_grad[half:], wq, ((1,), (1,)))
        )
    with jax.named_scope("norm1_back"):
        back1 = norm_backward(da1, hat1, inverse1, gain1)

    def split_width(x):
        return jnp.split(x, nrow, axis=1)

    with jax.named_scope("input_grad"):
        moved = grid.to_widths(split_width((back1 + back2).astype(LOW)))
        layer_input_grad = output_grad + jnp.concatenate(moved).astype(F32)

    with jax.named_scope("norm_params"):
        terms = jnp.stack(
            [jnp.sum(v, axis=0) for v in (da1 * hat1, da1, da2 * hat2, da2)]
        )
        terms = split_width(terms)
        terms = sum([grid.over_row(terms[k], k) for k in range(1, nrow)], terms[0])
        terms = terms + grid.over_core(terms)
        norm_params_grad = sum([grid.over_chip(terms, k) for k in range(1, grid.nz)], terms)

    with jax.named_scope("reduce_mlp"):
        mlp_sum = grid.reduce_col(
            dot(hidden[:half], wd, ((1,), (0,))), dot(hidden[half:], wd, ((1,), (0,)))
        )
    with jax.named_scope("block_output"):
        moved = grid.to_widths(split_width((attn_sum + mlp_sum).astype(LOW)))
        block_output = layer_input + jnp.concatenate(moved).astype(F32)

    with jax.named_scope("grad_down"):
        grad_down = grid.reduce_row(split_width(dot(hidden, out_full, ((0,), (0,)))))
    with jax.named_scope("grad_up"):
        grad_up = grid.reduce_row(jnp.split(dot(a2, pre_grad, ((0,), (0,))), nrow, axis=0))
    with jax.named_scope("grad_out"):
        grad_out = grid.reduce_row(split_width(dot(attended, middle_low, ((0,), (0,)))))
    with jax.named_scope("grad_qkv"):
        grad_qkv = grid.reduce_row(jnp.split(dot(a1, qkv_grad, ((0,), (0,))), nrow, axis=0))

    with jax.named_scope("adamw"):
        new_qkv, next_state_qkv = adamw(w_qkv, grad_qkv, state_qkv, DECAY)
        new_out, next_state_out = adamw(w_out, grad_out, state_out, DECAY)
        new_up, next_state_up = adamw(w_up, grad_up, state_up, DECAY)
        new_down, next_state_down = adamw(w_down, grad_down, state_down, DECAY)
        new_norms, next_state_norms = adamw(layernorm_params, norm_params_grad, state_norms, 0.0)
    return (
        block_output,
        layer_input_grad,
        grad_qkv,
        grad_out,
        grad_up,
        grad_down,
        norm_params_grad,
        new_qkv,
        new_out,
        new_up,
        new_down,
        new_norms,
        next_state_qkv,
        next_state_out,
        next_state_up,
        next_state_down,
        next_state_norms,
    )


def solution(mesh):
    tokens = P("col", "row")
    wide, tall = P("row", "col"), P("col", "row")
    return jax.shard_map(
        functools.partial(shards, mesh.shape["row"], mesh.shape["col"]),
        mesh=mesh,
        in_specs=(
            tokens,
            tokens,
            wide,
            tall,
            wide,
            tall,
            P(None, "row"),
            P(None, "row", "col"),
            P(None, "col", "row"),
            P(None, "row", "col"),
            P(None, "col", "row"),
            P(None, None, "row"),
            P("row", None),
        ),
        out_specs=(
            tokens,
            tokens,
            wide,
            tall,
            wide,
            tall,
            P(None, "row"),
            wide,
            tall,
            wide,
            tall,
            P(None, "row"),
            P(None, "row", "col"),
            P(None, "col", "row"),
            P(None, "row", "col"),
            P(None, "col", "row"),
            P(None, None, "row"),
        ),
        check_vma=False,
    )
```

```python
import functools
import math

import jax
import jax.numpy as jnp
from jax import lax
from jax.experimental import pallas as pl
from jax.experimental.pallas import tpu as pltpu
from jax.experimental.layout import Layout, with_layout_constraint
from jax.sharding import PartitionSpec as P

HS = 64
EPS_NORM = 1e-05
NEG_FILL = -1e30
BETA_ONE = 0.9
BETA_TWO = 0.95
RATE = 0.01
DECAY = 0.1
STEP_COUNT = 3
ADAM_EPS = 1e-08

LOW = jnp.bfloat16
F32 = jnp.float32


def dot(left, right, dims):
    return lax.dot_general(left, right, (dims, ((), ())), preferred_element_type=F32)


def row_major(x):
    return with_layout_constraint(x, Layout(major_to_minor=tuple(range(x.ndim))))


def after(x, *done):
    return lax.optimization_barrier((x, done))[0]


def select_xor(pieces, shift):
    count, bit = len(pieces), 1
    while bit < count:
        flag = (shift & bit) != 0
        pieces = [jnp.where(flag, pieces[i ^ bit], pieces[i]) for i in range(count)]
        bit *= 2
    return pieces


class Grid:
    def __init__(self, nrow, ncol):
        self.nrow, self.ncol, self.nz = nrow, ncol, ncol // 2
        self.row = lax.axis_index("row")
        self.col = lax.axis_index("col")
        self.lin = self.row * ncol + self.col

    def over_row(self, x, k):
        return lax.ppermute(x, "row", [(r, r ^ k) for r in range(self.nrow)])

    def over_chip(self, x, k):
        pairs = [(c, c ^ (2 * k)) for c in range(self.ncol)]
        return lax.ppermute(x, "col", pairs)

    def over_core(self, x):
        pairs = [(c, c ^ 1) for c in range(self.ncol)]
        return lax.ppermute(x, "col", pairs)

    def gather_row(self, x):
        return [x] + self.send_row([x] * (self.nrow - 1))

    def send_row(self, pieces):
        with jax.named_scope("rows"):
            return [self.over_row(piece, k) for k, piece in enumerate(pieces, 1)]

    def send_chips(self, pieces):
        with jax.named_scope("chips"):
            return [self.over_chip(piece, k) for k, piece in enumerate(pieces, 1)]

    def gather_col(self, x):
        own = [x] + self.send_chips([x] * (self.nz - 1))
        return own + [self.over_core(piece) for piece in own]

    def reduce_col(self, own, other):
        mine, *rest = share_core(own, self.over_core(other), self.nz)
        return [mine] + self.send_chips(rest)

    def to_tokens(self, pieces):
        sent = select_xor(pieces, self.row)
        got = []
        for m in range(self.nrow):
            pairs = [
                (r * self.ncol + c, c * self.nrow + (r ^ m))
                for r in range(self.nrow)
                for c in range(self.ncol)
            ]
            got.append(row_major(lax.ppermute(row_major(sent[m]), ("row", "col"), pairs)))
        return select_xor(got, (self.lin % self.nrow) ^ self.row)

    def to_widths(self, pieces):
        sent = select_xor(pieces, (self.lin % self.nrow) ^ self.row)
        got = []
        for m in range(self.nrow):
            pairs = [
                (c * self.nrow + (r ^ m), r * self.ncol + c)
                for r in range(self.nrow)
                for c in range(self.ncol)
            ]
            got.append(row_major(lax.ppermute(row_major(sent[m]), ("row", "col"), pairs)))
        return select_xor(got, self.row)


ANY = pl.BlockSpec(memory_space=pl.ANY)
VMEM = pl.BlockSpec(memory_space=pltpu.VMEM)


def run(body, name, outs, staged, plain, scratch=(), flops=0, spare=4):
    sizes = [x.size * x.dtype.itemsize for x in (*staged, *plain)]
    sizes += [o.size * o.dtype.itemsize for o in outs]
    held = sum(x.size * x.dtype.itemsize for x in (*plain, *outs))
    held += sum(math.prod(x.shape) * jnp.dtype(x.dtype).itemsize for x in scratch)
    return pl.pallas_call(
        body,
        name=name,
        out_shape=outs,
        in_specs=[ANY] * len(staged) + [VMEM] * len(plain),
        out_specs=[VMEM] * len(outs),
        scratch_shapes=[*scratch, pltpu.SemaphoreType.DMA((max(1, len(staged) * 2),))],
        compiler_params=pltpu.CompilerParams(vmem_limit_bytes=int(1.4 * held) + spare * 2**20),
        cost_estimate=pl.CostEstimate(
            flops=int(flops), bytes_accessed=int(sum(sizes)), transcendentals=0
        ),
    )(*staged, *plain)


def shape(dims, dtype):
    return jax.ShapeDtypeStruct(tuple(dims), dtype)


def stage(jobs, sem):
    copies = [pltpu.make_async_copy(s, t, sem.at[i]) for i, (s, t) in enumerate(jobs)]
    for copy in copies:
        copy.start()
    return copies


def stacked(pieces, target):
    rows = pieces[0].shape[0]
    return [(p, target.at[pl.ds(i * rows, rows)]) for i, p in enumerate(pieces)]


def wait(copies):
    for copy in copies:
        copy.wait()


def share_core(own, other, count):
    rows, width = own.shape
    part = rows // count

    def body(own_ref, other_ref, first_ref, *rest):
        *rest, _ = rest
        first_ref[...] = own_ref[:part, :] + other_ref[0].astype(F32)
        for k, ref in enumerate(rest, 1):
            total = own_ref[k * part : (k + 1) * part, :] + other_ref[k].astype(F32)
            ref[...] = total.astype(LOW)

    outs = [shape((part, width), F32)] + [shape((part, width), LOW)] * (count - 1)
    return run(body, "share_core", outs, (), (own, other))


def norm_first(mine, rows):
    width = mine.shape[1]

    def body(mine_ref, hat_ref, inverse_ref, out_ref, x_ref, params_ref, _):
        params = mine_ref[2 * rows :, :].astype(F32)
        params = params[:4] + params[4:8]
        params_ref[...] = params
        x = mine_ref[:rows, :].astype(F32)
        x_ref[...] = x
        hat, inverse = normalize(x)
        hat_ref[...] = hat
        inverse_ref[...] = jnp.broadcast_to(inverse, inverse_ref.shape)
        out_ref[...] = (hat * params[0:1] + params[1:2]).astype(LOW)

    outs = [
        shape((rows, width), F32),
        shape((rows, 128), F32),
        shape((rows, width), LOW),
        shape((rows, width), F32),
        shape((4, width), F32),
    ]
    return run(body, "norm_first", outs, (), (mine,))


def normalize(x):
    removed = x - jnp.mean(x, axis=1, keepdims=True)
    inverse = lax.rsqrt(jnp.mean(removed * removed, axis=1, keepdims=True) + EPS_NORM)
    return removed * inverse, inverse


def norm_second(parts, x, params):
    rows, width = x.shape

    def body(*refs):
        *parts, x_ref, params_ref, hat_ref, inverse_ref, out_ref, sum_ref, _ = refs
        total = sum([p[...].astype(F32) for p in parts[1:]], parts[0][...])
        sum_ref[...] = total
        hat, inverse = normalize(x_ref[...] + total)
        hat_ref[...] = hat
        inverse_ref[...] = jnp.broadcast_to(inverse, inverse_ref.shape)
        out_ref[...] = (hat * params_ref[2:3, :] + params_ref[3:4, :]).astype(LOW)

    outs = [
        shape((rows, width), F32),
        shape((rows, 128), F32),
        shape((rows, width), LOW),
        shape((rows, width), F32),
    ]
    return run(body, "norm_second", outs, (), (*parts, x, params))


def norm_back(parts, hat, inverse, params, index, extra):
    rows, width = hat.shape

    def body(*refs):
        *parts, hat_ref, inverse_ref, params_ref, extra_ref, low_ref, back_ref, terms_ref, _ = refs
        incoming = sum([p[...].astype(F32) for p in parts[1:]], parts[0][...])
        hat = hat_ref[...]
        scaled = incoming * params_ref[index : index + 1, :]
        first = jnp.mean(scaled, axis=1, keepdims=True)
        second = jnp.mean(scaled * hat, axis=1, keepdims=True)
        back = inverse_ref[:, 0:1] * (scaled - first - hat * second)
        back_ref[...] = back
        low_ref[...] = (back + extra_ref[...].astype(F32)).astype(LOW)
        terms_ref[0:1, :] = jnp.sum(incoming * hat, axis=0, keepdims=True)
        terms_ref[1:2, :] = jnp.sum(incoming, axis=0, keepdims=True)

    outs = [shape((rows, width), LOW), shape((rows, width), F32), shape((2, width), F32)]
    return run(body, "norm_back", outs, (), (*parts, hat, inverse, params, extra))


def matmul(left, right):
    return dot(left, right, ((1,), (0,)))


def matmul_t(left, right):
    return dot(left, right, ((1,), (1,)))


def t_matmul(left, right):
    return dot(left, right, ((0,), (0,)))


def halves_out(read, weight, own_ref, other_ref):
    half = own_ref.shape[0]
    other_ref[...] = matmul_t(read(half, half), weight).astype(LOW).reshape(other_ref.shape)
    own_ref[...] = matmul_t(read(0, half), weight)


def attention_forward(acts, wq, wo, spots_col, spots_row):
    count, groups = len(acts), len(wq)
    rows, width = acts[0].shape
    tokens, wide = rows * count, wq[0].shape[1]
    heads = wide // (3 * HS)

    def body(*refs):
        acts, refs = refs[:count], refs[count:]
        wq, refs = refs[:groups], refs[groups:]
        wo, refs = refs[:groups], refs[groups:]
        col_ref, row_ref, qkv_ref, lse_ref, att_ref, own_ref, other_ref = refs[:7]
        a_s, wq_s, wo_s, mask_s, sem = refs[7:]
        copies = stage(stacked(acts, a_s) + stacked(wq, wq_s) + stacked(wo, wo_s), sem)
        mask_s[...] = (
            (row_ref[0:1, :] <= col_ref[:, 0:1]) & (row_ref[1:2, :] == col_ref[:, 1:2])
        ).astype(F32)
        wait(copies)
        block = tokens // 4

        def project(i, carry):
            at = pl.ds(pl.multiple_of(i * block, block), block)
            qkv_ref[at, :] = matmul(a_s[at, :], wq_s[...]).astype(LOW)
            return carry

        lax.fori_loop(0, 4, project, 0)
        lane = lax.broadcasted_iota(jnp.int32, (tokens, 128), 1)
        lse_all = jnp.zeros((tokens, 128), F32)
        for h in range(heads):
            at = 3 * HS * h
            q = qkv_ref[:, at : at + HS]
            k = qkv_ref[:, at + HS : at + 2 * HS]
            v = qkv_ref[:, at + 2 * HS : at + 3 * HS]
            scores = matmul_t(q, k) * HS ** (-0.5)
            scores = jnp.where(mask_s[...] > 0, scores, NEG_FILL)
            top = jnp.max(scores, axis=1, keepdims=True)
            weights = jnp.exp(scores - top)
            total = jnp.sum(weights, axis=1, keepdims=True)
            lse_all = jnp.where(lane == h, top + jnp.log(total), lse_all)
            probs = (weights / total).astype(LOW)
            att_ref[:, h * HS : (h + 1) * HS] = matmul(probs, v).astype(LOW)
        lse_ref[...] = lse_all
        halves_out(lambda o, n: att_ref[o : o + n, :], wo_s[...], own_ref, other_ref)

    outs = [
        shape((tokens, wide), LOW),
        shape((tokens, 128), F32),
        shape((tokens, heads * HS), LOW),
        shape((tokens // 2, width), F32),
        shape((count // 2, rows, width), LOW),
    ]
    scratch = [
        pltpu.VMEM((tokens, width), LOW),
        pltpu.VMEM((width, wide), LOW),
        pltpu.VMEM((width, heads * HS), LOW),
        pltpu.VMEM((tokens, tokens), F32),
    ]
    flops = 2 * tokens * width * (wide + heads * HS) + 4 * heads * tokens * tokens * HS
    return run(
        body,
        "attention_forward",
        outs,
        (*acts, *wq, *wo),
        (spots_col, spots_row),
        scratch,
        flops,
        spare=16,
    )


def attention_backward(acts, wq, wo, qkv, lse, spots_col, spots_row):
    count, groups = len(acts), len(wq)
    rows, width = acts[0].shape
    tokens, wide = rows * count, wq[0].shape[1]
    heads = wide // (3 * HS)

    def body(*refs):
        acts, refs = refs[:count], refs[count:]
        wq, refs = refs[:groups], refs[groups:]
        wo, refs = refs[:groups], refs[groups:]
        qkv_ref, lse_ref, col_ref, row_ref, grad_ref, own_ref, other_ref = refs[:7]
        a_s, wq_s, wo_s, mask_s, in_s, sem = refs[7:]
        copies = stage(stacked(acts, a_s) + stacked(wq, wq_s) + stacked(wo, wo_s), sem)
        mask_s[...] = (
            (row_ref[0:1, :] <= col_ref[:, 0:1]) & (row_ref[1:2, :] == col_ref[:, 1:2])
        ).astype(F32)
        wait(copies)
        in_s[...] = matmul(a_s[...], wo_s[...]).astype(LOW)
        for h in range(heads):
            at = 3 * HS * h
            q = qkv_ref[:, at : at + HS]
            k = qkv_ref[:, at + HS : at + 2 * HS]
            v = qkv_ref[:, at + 2 * HS : at + 3 * HS]
            up = in_s[:, h * HS : (h + 1) * HS]
            scores = matmul_t(q, k) * HS ** (-0.5)
            scores = jnp.where(mask_s[...] > 0, scores, NEG_FILL)
            probs = jnp.exp(scores - lse_ref[:, h : h + 1])
            dprobs = matmul_t(up, v)
            delta = jnp.sum(probs * dprobs, axis=1, keepdims=True)
            dscores = (probs * (dprobs - delta)).astype(LOW)
            grad_ref[:, at : at + HS] = (matmul(dscores, k) * HS ** (-0.5)).astype(LOW)
            grad_ref[:, at + HS : at + 2 * HS] = (
                t_matmul(dscores, q) * HS ** (-0.5)
            ).astype(LOW)
            grad_ref[:, at + 2 * HS : at + 3 * HS] = t_matmul(probs.astype(LOW), up).astype(LOW)
        halves_out(lambda o, n: grad_ref[o : o + n, :], wq_s[...], own_ref, other_ref)

    outs = [
        shape((tokens, wide), LOW),
        shape((tokens // 2, width), F32),
        shape((count // 2, rows, width), LOW),
    ]
    scratch = [
        pltpu.VMEM((tokens, width), LOW),
        pltpu.VMEM((width, wide), LOW),
        pltpu.VMEM((width, heads * HS), LOW),
        pltpu.VMEM((tokens, tokens), F32),
        pltpu.VMEM((tokens, heads * HS), LOW),
    ]
    flops = 2 * tokens * width * (wide + heads * HS) + 10 * heads * tokens * tokens * HS
    return run(
        body,
        "attention_backward",
        outs,
        (*acts, *wq, *wo),
        (qkv, lse, spots_col, spots_row),
        scratch,
        flops,
        spare=16,
    )


CURVE = (2.0 / 3.141592653589793) ** 0.5
CUBE = 0.044715


def two_weights(pieces, up_s, down_s):
    rows = pieces[0].shape[0] // 2
    jobs = []
    for i, piece in enumerate(pieces):
        jobs.append((piece.at[pl.ds(0, rows)], up_s.at[pl.ds(i * rows, rows)]))
        jobs.append((piece.at[pl.ds(rows, rows)], down_s.at[pl.ds(i * rows, rows)]))
    return jobs


def mlp_middle(acts, outer, weights):
    count, groups = len(acts), len(weights)
    rows, width = acts[0].shape
    tokens, wide = rows * count, weights[0].shape[1]

    def body(*refs):
        acts, refs = refs[:count], refs[count:]
        outer, refs = refs[:count], refs[count:]
        weights, refs = refs[:groups], refs[groups:]
        hidden_ref, grad_ref, own_ref, other_ref, a_s, o_s, up_s, down_s, sem = refs
        jobs = stacked(acts, a_s) + stacked(outer, o_s) + two_weights(weights, up_s, down_s)
        wait(stage(jobs, sem))
        block = tokens // 4

        def step(i, carry):
            at = pl.ds(pl.multiple_of(i * block, block), block)
            pre = matmul(a_s[at, :], up_s[...])
            upper = matmul(o_s[at, :], down_s[...])
            square = pre * pre
            bent = jnp.tanh(CURVE * (pre + CUBE * square * pre))
            hidden_ref[at, :] = (0.5 * pre * (1.0 + bent)).astype(LOW)
            rate = 0.5 * (1.0 + bent) + 0.5 * pre * (1.0 - bent * bent) * (
                CURVE * (1.0 + 3.0 * CUBE * square)
            )
            grad_ref[at, :] = (rate * upper).astype(LOW)
            return carry

        lax.fori_loop(0, 4, step, 0)
        halves_out(lambda o, n: grad_ref[o : o + n, :], up_s[...], own_ref, other_ref)

    outs = [
        shape((tokens, wide), LOW),
        shape((tokens, wide), LOW),
        shape((tokens // 2, width), F32),
        shape((count // 2, rows, width), LOW),
    ]
    scratch = [
        pltpu.VMEM((tokens, width), LOW),
        pltpu.VMEM((tokens, width), LOW),
        pltpu.VMEM((width, wide), LOW),
        pltpu.VMEM((width, wide), LOW),
    ]
    flops = 6 * tokens * width * wide
    return run(body, "mlp_middle", outs, (*acts, *outer, *weights), (), scratch, flops)


def mlp_out(hidden, weights, count):
    groups = len(weights)
    tokens, wide = hidden.shape
    half_rows = weights[0].shape[0] // 2
    width = half_rows * groups

    def body(*refs):
        weights, refs = refs[:groups], refs[groups:]
        hidden_ref, own_ref, other_ref, down_s, sem = refs
        jobs = [
            (w.at[pl.ds(half_rows, half_rows)], down_s.at[pl.ds(i * half_rows, half_rows)])
            for i, w in enumerate(weights)
        ]
        wait(stage(jobs, sem))
        halves_out(lambda o, n: hidden_ref[o : o + n, :], down_s[...], own_ref, other_ref)

    outs = [
        shape((tokens // 2, width), F32),
        shape((count, tokens // 2 // count, width), LOW),
    ]
    scratch = [pltpu.VMEM((width, wide), LOW)]
    flops = 2 * tokens * width * wide
    return run(body, "mlp_out", outs, weights, (hidden,), scratch, flops)


def weight_grads(first, first_grad, second, second_grad, groups, beside):
    count = len(first)
    rows, width = first[0].shape
    tokens, part = rows * count, width // groups
    wide, wide2 = first_grad.shape[1], second_grad.shape[1]
    spot = (0, wide) if beside else (part, 0)
    dims = (part, wide + wide2) if beside else (2 * part, wide)

    def body(*refs):
        first, refs = refs[:count], refs[count:]
        second, refs = refs[:count], refs[count:]
        grad_ref, grad2_ref, own_ref, *rest, a_s, b_s, prod_s, prod2_s, sem = refs
        copies = stage(stacked(first, a_s) + stacked(second, b_s), sem)
        wait(copies[:count])
        prod_s[...] = t_matmul(a_s[...], grad_ref[...])
        wait(copies[count:])
        prod2_s[...] = t_matmul(b_s[...], grad2_ref[...])
        for k, ref in enumerate((own_ref, *rest)):
            one = prod_s[k * part : (k + 1) * part, :].astype(ref.dtype)
            two = prod2_s[k * part : (k + 1) * part, :].astype(ref.dtype)
            ref[0:part, 0:wide] = one
            ref[spot[0] : spot[0] + part, spot[1] : spot[1] + wide2] = two

    outs = [shape(dims, F32)] + [shape(dims, LOW)] * (groups - 1)
    scratch = [
        pltpu.VMEM((tokens, width), LOW),
        pltpu.VMEM((tokens, width), LOW),
        pltpu.VMEM((width, wide), F32),
        pltpu.VMEM((width, wide2), F32),
    ]
    flops = 2 * tokens * width * (wide + wide2)
    return run(
        body, "weight_grads", outs, (*first, *second), (first_grad, second_grad), scratch, flops
    )


def step_rule(param, grad, first, second, decay):
    first = BETA_ONE * first + (1.0 - BETA_ONE) * grad
    second = BETA_TWO * second + (1.0 - BETA_TWO) * grad * grad
    first_hat = first / (1.0 - BETA_ONE**STEP_COUNT)
    second_hat = second / (1.0 - BETA_TWO**STEP_COUNT)
    updated = param - RATE * (first_hat / (jnp.sqrt(second_hat) + ADAM_EPS) + decay * param)
    return updated, first, second


def adamw(param, grad, state, decay):
    updated, first, second = step_rule(param, grad, state[0], state[1], decay)
    return updated, jnp.stack([first, second])


def update_two(parts, param, state, param2, state2, beside):
    part, wide = param.shape
    wide2 = param2.shape[1]
    count = len(parts)
    spot = (0, wide) if beside else (part, 0)

    def body(*refs):
        parts, refs = refs[:count], refs[count:]
        ins, outs = refs[:4], refs[4:10]
        for i, (row, col, size) in enumerate(((0, 0, wide), (*spot, wide2))):
            param_ref, state_ref = ins[2 * i : 2 * i + 2]
            grad_ref, new_ref, next_ref = outs[3 * i : 3 * i + 3]
            grad = sum(
                [p[row : row + part, col : col + size].astype(F32) for p in parts[1:]],
                parts[0][row : row + part, col : col + size],
            )
            grad_ref[...] = grad
            new_ref[...], next_ref[0], next_ref[1] = step_rule(
                param_ref[...], grad, state_ref[0], state_ref[1], DECAY
            )

    outs = []
    for size in (wide, wide2):
        outs += [shape((part, size), F32)] * 2 + [shape((2, part, size), F32)]
    return run(body, "update_two", outs, (), (*parts, param, state, param2, state2))


def shards(
    nrow,
    ncol,
    layer_input,
    output_grad,
    w_qkv,
    w_out,
    w_up,
    w_down,
    layernorm_params,
    state_qkv,
    state_out,
    state_up,
    state_down,
    state_norms,
    segment_ids,
):
    grid = Grid(nrow, ncol)
    own_tokens = layer_input.shape[0] // nrow
    row_tokens = own_tokens * ncol

    def split_rows(x):
        return jnp.split(x, nrow, axis=0)

    def split_width(x):
        return jnp.split(x, nrow, axis=1)

    with jax.named_scope("to_tokens"):
        high = lax.reduce_precision(layernorm_params, 8, 7)
        params_low = jnp.concatenate([high, layernorm_params - high]).astype(LOW)
        pieces = [
            jnp.concatenate([x, g, params_low])
            for x, g in zip(
                split_rows(layer_input.astype(LOW)), split_rows(output_grad.astype(LOW))
            )
        ]
        mine = jnp.concatenate(grid.to_tokens(pieces), axis=1)
        out_low = mine[own_tokens : 2 * own_tokens]
    with jax.named_scope("norm1"):
        hat1, inverse1, a1_own, x, params = norm_first(mine, own_tokens)
    block = w_qkv.shape[0]

    def tidy(pieces):
        if block % 16 == 0:
            return pieces
        parts = range(0, pieces[0].shape[0], block)
        return [jnp.concatenate([p[at : at + block] for at in parts for p in pieces])]

    with jax.named_scope("weights_qkv"):
        wq = tidy(grid.gather_row(w_qkv.astype(LOW)))
    with jax.named_scope("weights_out"):
        wo = tidy(grid.gather_row(w_out.T.astype(LOW)))
    with jax.named_scope("weights_mlp"):
        w_mlp = jnp.concatenate([w_up.astype(LOW), w_down.T.astype(LOW)])
        w_mlp = tidy(grid.gather_row(after(w_mlp, wq)))

    with jax.named_scope("mask"):
        chip, core = grid.col // 2, grid.col % 2
        spot = jnp.arange(row_tokens)
        sequence = spot // segment_ids.shape[1]
        marks = sequence * (1 + jnp.max(segment_ids)) + segment_ids.reshape(-1)

        def reorder(values):
            values = values.reshape(grid.nz, 2, own_tokens)
            chips = select_xor([values[z] for z in range(grid.nz)], chip)
            cores = select_xor([jnp.stack([v[h] for v in chips]) for h in range(2)], core)
            return jnp.concatenate(cores).reshape(-1)

        spots_row = jnp.stack([reorder(spot), reorder(marks)])
        spots_col = spots_row.T

    with jax.named_scope("gather_a1"):
        a1 = grid.gather_col(a1_own)
    with jax.named_scope("gather_out"):
        out_full = grid.gather_col(after(out_low, a1[: grid.nz]))
    with jax.named_scope("attend"):
        qkv, lse, attended, *partial_sums = attention_forward(a1, wq, wo, spots_col, spots_row)
    with jax.named_scope("reduce_attn"):
        parts = grid.reduce_col(*partial_sums)
    with jax.named_scope("norm2"):
        hat2, inverse2, a2_own, attn_sum = norm_second(parts, x, params)
    with jax.named_scope("gather_a2"):
        a2 = grid.gather_col(a2_own)
    with jax.named_scope("up"):
        hidden, pre_grad, *partial_sums = mlp_middle(a2, out_full, w_mlp)
    with jax.named_scope("reduce_da2"):
        parts = grid.reduce_col(*partial_sums)
    with jax.named_scope("grad_mlp"):
        mine, *rest = weight_grads(
            a2, after(pre_grad, parts[0]), out_full, hidden, nrow, beside=False
        )
        mlp_parts = [mine] + grid.send_row(rest)
    with jax.named_scope("norm2_back"):
        middle_low_own, back2, terms2 = norm_back(parts, hat2, inverse2, params, 2, out_low)
    with jax.named_scope("gather_mid"):
        middle_low = grid.gather_col(middle_low_own)
    with jax.named_scope("reduce_mlp"):
        own, other = mlp_out(after(hidden, middle_low_own), w_mlp, grid.nz)
        own = after(own, middle_low[: grid.nz])
        mlp_parts_out = grid.reduce_col(own, other)
        mlp_sum = sum([p.astype(F32) for p in mlp_parts_out[1:]], mlp_parts_out[0])
        out_delta = (attn_sum + mlp_sum).astype(LOW)
    with jax.named_scope("attend_back"):
        qkv_grad, *partial_sums = attention_backward(
            middle_low, wq, wo, qkv, lse, spots_col, spots_row
        )
    with jax.named_scope("reduce_da1"):
        parts = grid.reduce_col(*partial_sums)
    with jax.named_scope("grad_attn"):
        mine, *rest = weight_grads(
            a1, after(qkv_grad, parts[0]), middle_low, attended, nrow, beside=True
        )
        attn_parts = [mine] + grid.send_row(rest)
    with jax.named_scope("norm1_back"):
        input_delta, _, terms1 = norm_back(parts, hat1, inverse1, params, 0, back2)
    with jax.named_scope("to_widths"):
        terms = jnp.concatenate([terms1, terms2])
        high = lax.reduce_precision(terms, 8, 7)
        message = jnp.concatenate(
            [input_delta, out_delta, high.astype(LOW), (terms - high).astype(LOW)]
        )
        moved = grid.to_widths(split_width(message))
        layer_input_grad = output_grad + jnp.concatenate([p[:own_tokens] for p in moved]).astype(F32)
        block_output = layer_input + jnp.concatenate(
            [p[own_tokens : 2 * own_tokens] for p in moved]
        ).astype(F32)
    with jax.named_scope("norm_params"):
        terms = sum(p[2 * own_tokens :].astype(F32) for p in moved)
        terms = terms[:4] + terms[4:]
        terms = terms + grid.over_core(terms)
        norm_params_grad = sum(grid.send_chips([terms] * (grid.nz - 1)), terms)

    def flip(x):
        return jnp.swapaxes(x, -1, -2)

    with jax.named_scope("adamw_mlp"):
        grad_up, new_up, next_state_up, *rest = update_two(
            mlp_parts, w_up, state_up, flip(w_down), flip(state_down), beside=False
        )
        grad_down, new_down, next_state_down = map(flip, rest)
    with jax.named_scope("adamw_attn"):
        grad_qkv, new_qkv, next_state_qkv, *rest = update_two(
            attn_parts, w_qkv, state_qkv, flip(w_out), flip(state_out), beside=True
        )
        grad_out, new_out, next_state_out = map(flip, rest)
    with jax.named_scope("adamw_norms"):
        new_norms, next_state_norms = adamw(layernorm_params, norm_params_grad, state_norms, 0.0)
    return (
        block_output,
        layer_input_grad,
        grad_qkv,
        grad_out,
        grad_up,
        grad_down,
        norm_params_grad,
        new_qkv,
        new_out,
        new_up,
        new_down,
        new_norms,
        next_state_qkv,
        next_state_out,
        next_state_up,
        next_state_down,
        next_state_norms,
    )


def solution(mesh):
    tokens = P("col", "row")
    wide, tall = P("row", "col"), P("col", "row")
    return jax.shard_map(
        functools.partial(shards, mesh.shape["row"], mesh.shape["col"]),
        mesh=mesh,
        in_specs=(
            tokens,
            tokens,
            wide,
            tall,
            wide,
            tall,
            P(None, "row"),
            P(None, "row", "col"),
            P(None, "col", "row"),
            P(None, "row", "col"),
            P(None, "col", "row"),
            P(None, None, "row"),
            P("row", None),
        ),
        out_specs=(
            tokens,
            tokens,
            wide,
            tall,
            wide,
            tall,
            P(None, "row"),
            wide,
            tall,
            wide,
            tall,
            P(None, "row"),
            P(None, "row", "col"),
            P(None, "col", "row"),
            P(None, "row", "col"),
            P(None, "col", "row"),
            P(None, None, "row"),
        ),
        check_vma=False,
    )
```

```python
import math

import jax
import jax.numpy as jnp
from jax import lax
from jax.experimental import pallas as pl
from jax.experimental.pallas import tpu as pltpu
from jax.sharding import PartitionSpec as P


HS = 64
EPS_NORM = 1e-05
NEG_FILL = -1e30
BETA_ONE = 0.9
BETA_TWO = 0.95
RATE = 0.01
DECAY = 0.1
STEP_COUNT = 3
ADAM_EPS = 1e-08

LOW = jnp.bfloat16
F32 = jnp.float32


def dot(left, right, dims):
    return lax.dot_general(left, right, (dims, ((), ())), preferred_element_type=F32)


def after(x, *done):
    return lax.optimization_barrier((x, done))[0]


def select_xor(pieces, shift):
    count, bit = len(pieces), 1
    while bit < count:
        flag = (shift & bit) != 0
        pieces = [jnp.where(flag, pieces[i ^ bit], pieces[i]) for i in range(count)]
        bit *= 2
    return pieces


class Grid:
    def __init__(self, nrow, ncol):
        self.nrow, self.ncol, self.nz = nrow, ncol, ncol // 2
        self.row = lax.axis_index("row")
        self.col = lax.axis_index("col")
        self.lin = self.row * ncol + self.col

    def over_row(self, x, k):
        return lax.ppermute(x, "row", [(r, r ^ k) for r in range(self.nrow)])

    def over_chip(self, x, k):
        pairs = [(c, c ^ (2 * k)) for c in range(self.ncol)]
        return lax.ppermute(x, "col", pairs)

    def over_core(self, x):
        pairs = [(c, c ^ 1) for c in range(self.ncol)]
        return lax.ppermute(x, "col", pairs)

    def gather_row(self, x):
        return [x] + self.send_row([x] * (self.nrow - 1))

    def send_row(self, pieces):
        sent = []
        for k, piece in enumerate(pieces, 1):
            sent.append(self.over_row(piece, k))
        return sent

    def send_chips(self, pieces):
        return [self.over_chip(piece, k) for k, piece in enumerate(pieces, 1)]

    def gather_col(self, x):
        own = [x] + self.send_chips([x] * (self.nz - 1))
        return own + [self.over_core(piece) for piece in own]

    def reduce_col(self, own, other):
        mine, *rest = share_core(own, self.over_core(other), self.nz)
        return [mine] + self.send_chips(rest)

    def to_tokens(self, pieces):
        got = []
        for m in range(self.nrow):
            pairs = [
                (r * self.ncol + c, c * self.nrow + (r ^ m))
                for r in range(self.nrow)
                for c in range(self.ncol)
            ]
            got.append(lax.ppermute(pieces[m], ("row", "col"), pairs))
        return got

    def to_widths(self, pieces):
        got = []
        for m in range(self.nrow):
            pairs = [
                (c * self.nrow + (r ^ m), r * self.ncol + c)
                for r in range(self.nrow)
                for c in range(self.ncol)
            ]
            got.append(lax.ppermute(pieces[m], ("row", "col"), pairs))
        return got


ANY = pl.BlockSpec(memory_space=pl.ANY)
VMEM = pl.BlockSpec(memory_space=pltpu.VMEM)


SMEM = pl.BlockSpec(memory_space=pltpu.SMEM)


def run(body, outs, staged, plain, scratch=(), flops=0, spare=4, scalars=()):
    sizes = [x.size * x.dtype.itemsize for x in (*staged, *plain)]
    sizes += [o.size * o.dtype.itemsize for o in outs]
    held = sum(x.size * x.dtype.itemsize for x in (*plain, *outs))
    held += sum(math.prod(x.shape) * jnp.dtype(x.dtype).itemsize for x in scratch)
    return pl.pallas_call(
        body,
        out_shape=outs,
        in_specs=[SMEM] * len(scalars) + [ANY] * len(staged) + [VMEM] * len(plain),
        out_specs=[VMEM] * len(outs),
        scratch_shapes=[*scratch, pltpu.SemaphoreType.DMA((max(1, len(staged) * 2),))],
        compiler_params=pltpu.CompilerParams(vmem_limit_bytes=int(1.4 * held) + spare * 2**20),
        cost_estimate=pl.CostEstimate(
            flops=int(flops), bytes_accessed=int(sum(sizes)), transcendentals=0
        ),
    )(*[x.reshape(1) for x in scalars], *staged, *plain)


def shape(dims, dtype):
    return jax.ShapeDtypeStruct(tuple(dims), dtype)


def stage(jobs, sem):
    copies = [pltpu.make_async_copy(s, t, sem.at[i]) for i, (s, t) in enumerate(jobs)]
    for copy in copies:
        copy.start()
    return copies


def stacked(pieces, target):
    rows = pieces[0].shape[0]
    return [(p, target.at[pl.ds(i * rows, rows)]) for i, p in enumerate(pieces)]


def wait(copies):
    for copy in copies:
        copy.wait()


def share_core(own, other, count):
    rows, width = own.shape
    part = rows // count

    def body(own_ref, other_ref, first_ref, *rest):
        *rest, _ = rest
        first_ref[...] = own_ref[:part, :] + other_ref[0].astype(F32)
        for k, ref in enumerate(rest, 1):
            total = own_ref[k * part : (k + 1) * part, :] + other_ref[k].astype(F32)
            ref[...] = total.astype(LOW)

    outs = [shape((part, width), F32)] + [shape((part, width), LOW)] * (count - 1)
    return run(body, outs, (), (own, other))


def split_terms(values):
    high = values.astype(LOW).astype(F32)
    return jnp.concatenate([high, values - high], axis=0).astype(LOW)


def entry(row, x_t, grad_t, params, count):
    width, tokens = x_t.shape
    rows = tokens // count

    def body(row_ref, x_ref, grad_ref, params_ref, *refs):
        *outs, x_s, grad_s, _ = refs
        x_s[...] = x_ref[...].T
        grad_s[...] = grad_ref[...].T
        tail = split_terms(params_ref[...])
        for m, ref in enumerate(outs):
            at = pl.ds(pl.multiple_of((row_ref[0] ^ m) * rows, rows), rows)
            ref[0:rows, :] = x_s[at, :].astype(LOW)
            ref[rows : 2 * rows, :] = grad_s[at, :].astype(LOW)
            ref[2 * rows :, :] = tail

    outs = [shape((2 * rows + 8, width), LOW)] * count
    scratch = [pltpu.VMEM((tokens, width), F32)] * 2
    return run(body, outs, (), (x_t, grad_t, params), scratch, scalars=(row,))


def norm_first(shift, pieces, rows):
    count = len(pieces)
    length, part = pieces[0].shape
    width = part * count

    def body(shift_ref, *refs):
        pieces, refs = refs[:count], refs[count:]
        hat_ref, inverse_ref, out_ref, x_ref, grad_ref, params_ref, held_s, all_s, _ = refs
        for i, piece in enumerate(pieces):
            held_s[i] = piece[...].astype(F32)
        for k in range(count):
            all_s[:, k * part : (k + 1) * part] = held_s[shift_ref[0] ^ k]
        params = all_s[2 * rows : 2 * rows + 4, :] + all_s[2 * rows + 4 : 2 * rows + 8, :]
        params_ref[...] = params
        grad_ref[...] = all_s[rows : 2 * rows, :].astype(LOW)
        x = all_s[0:rows, :]
        x_ref[...] = x
        hat, inverse = normalize(x)
        hat_ref[...] = hat
        inverse_ref[...] = jnp.broadcast_to(inverse, inverse_ref.shape)
        out_ref[...] = (hat * params[0:1] + params[1:2]).astype(LOW)

    outs = [
        shape((rows, width), F32),
        shape((rows, 128), F32),
        shape((rows, width), LOW),
        shape((rows, width), F32),
        shape((rows, width), LOW),
        shape((4, width), F32),
    ]
    scratch = [pltpu.VMEM((count, length, part), F32), pltpu.VMEM((length, width), F32)]
    return run(body, outs, (), pieces, scratch, scalars=(shift,))


def normalize(x):
    removed = x - jnp.mean(x, axis=1, keepdims=True)
    inverse = lax.rsqrt(jnp.mean(removed * removed, axis=1, keepdims=True) + EPS_NORM)
    return removed * inverse, inverse


def norm_second(parts, x, params):
    rows, width = x.shape

    def body(*refs):
        *parts, x_ref, params_ref, hat_ref, inverse_ref, out_ref, sum_ref, _ = refs
        total = sum([p[...].astype(F32) for p in parts[1:]], parts[0][...])
        sum_ref[...] = total
        hat, inverse = normalize(x_ref[...] + total)
        hat_ref[...] = hat
        inverse_ref[...] = jnp.broadcast_to(inverse, inverse_ref.shape)
        out_ref[...] = (hat * params_ref[2:3, :] + params_ref[3:4, :]).astype(LOW)

    outs = [
        shape((rows, width), F32),
        shape((rows, 128), F32),
        shape((rows, width), LOW),
        shape((rows, width), F32),
    ]
    return run(body, outs, (), (*parts, x, params))


def back_through(parts, hat_ref, inverse_ref, gain):
    incoming = sum([p[...].astype(F32) for p in parts[1:]], parts[0][...])
    hat = hat_ref[...]
    scaled = incoming * gain
    first = jnp.mean(scaled, axis=1, keepdims=True)
    second = jnp.mean(scaled * hat, axis=1, keepdims=True)
    back = inverse_ref[:, 0:1] * (scaled - first - hat * second)
    terms = [jnp.sum(v, axis=0, keepdims=True) for v in (incoming * hat, incoming)]
    return back, jnp.concatenate(terms, axis=0)


def norm_second_back(parts, hat, inverse, params, grad):
    rows, width = hat.shape

    def body(*refs):
        *parts, hat_ref, inverse_ref, params_ref, grad_ref, low_ref, back_ref, terms_ref, _ = refs
        back, terms_ref[...] = back_through(parts, hat_ref, inverse_ref, params_ref[2:3, :])
        back_ref[...] = back
        low_ref[...] = (back + grad_ref[...].astype(F32)).astype(LOW)

    outs = [shape((rows, width), LOW), shape((rows, width), F32), shape((2, width), F32)]
    return run(body, outs, (), (*parts, hat, inverse, params, grad))


def norm_first_back(shift, parts, hat, inverse, params, back2, terms2, out_parts, count):
    rows, width = hat.shape
    part = width // count
    pieces = len(parts)

    def body(shift_ref, *refs):
        parts, refs = refs[:pieces], refs[pieces:]
        out_parts, refs = refs[: pieces + 1], refs[pieces + 1 :]
        hat_ref, inverse_ref, params_ref, back2_ref, terms2_ref = refs[:5]
        *outs, terms_ref, held_s, _ = refs[5:]
        back, terms1 = back_through(parts, hat_ref, inverse_ref, params_ref[0:1, :])
        delta = (back + back2_ref[...]).astype(LOW)
        out_delta = sum(p[...].astype(F32) for p in out_parts).astype(LOW)
        terms = jnp.concatenate([terms1, terms2_ref[...]], axis=0)
        for k in range(count):
            at = slice(k * part, (k + 1) * part)
            terms_ref[k] = terms[:, at]
            held_s[k, 0:rows] = delta[:, at].astype(F32)
            held_s[k, rows : 2 * rows] = out_delta[:, at].astype(F32)
        for m, ref in enumerate(outs):
            ref[...] = held_s[shift_ref[0] ^ m].astype(LOW)

    outs = [shape((2 * rows, part), LOW)] * count + [shape((count, 4, part), F32)]
    scratch = [pltpu.VMEM((count, 2 * rows, part), F32)]
    plain = (*parts, *out_parts, hat, inverse, params, back2, terms2)
    return run(body, outs, (), plain, scratch, scalars=(shift,))


def leave(row, pieces, x_t, grad_t):
    count = len(pieces)
    length, width = pieces[0].shape
    rows = length // 2

    def body(row_ref, *refs):
        pieces, refs = refs[:count], refs[count:]
        x_ref, grad_ref, input_ref, block_ref, held_s, one_s, two_s, _ = refs
        for i, piece in enumerate(pieces):
            held_s[i] = piece[...].astype(F32)
        for p in range(count):
            one_s[p * rows : (p + 1) * rows, :] = held_s[row_ref[0] ^ p, 0:rows]
            two_s[p * rows : (p + 1) * rows, :] = held_s[row_ref[0] ^ p, rows : 2 * rows]
        input_ref[...] = grad_ref[...] + one_s[...].T
        block_ref[...] = x_ref[...] + two_s[...].T

    outs = [shape(x_t.shape, F32)] * 2
    scratch = [pltpu.VMEM((count, length, width), F32)]
    scratch += [pltpu.VMEM((rows * count, width), F32)] * 2
    return run(body, outs, (), (*pieces, x_t, grad_t), scratch, scalars=(row,))


def matmul(left, right):
    return dot(left, right, ((1,), (0,)))


def matmul_t(left, right):
    return dot(left, right, ((1,), (1,)))


def t_matmul(left, right):
    return dot(left, right, ((0,), (0,)))


def halves_out(read, weight, own_ref, other_ref):
    half = own_ref.shape[0]
    other_ref[...] = matmul_t(read(half, half), weight).astype(LOW).reshape(other_ref.shape)
    own_ref[...] = matmul_t(read(0, half), weight)


def attention_forward(acts, weights, spots):
    count, groups = len(acts), len(weights)
    rows, width = acts[0].shape
    tokens, wide = rows * count, weights[0].shape[1]
    heads = wide // (3 * HS)

    def body(*refs):
        acts, refs = refs[:count], refs[count:]
        weights, refs = refs[:groups], refs[groups:]
        row_ref, qkv_ref, lse_ref, att_ref, a_s, wq_s, mask_s, sem = refs
        copies = stage(stacked(acts, a_s) + stacked(weights, wq_s), sem)
        spots = row_ref[...]
        turned = spots.T
        mask_s[...] = (
            (spots[0:1, :] <= turned[:, 0:1]) & (spots[1:2, :] == turned[:, 1:2])
        ).astype(F32)
        wait(copies)
        qkv_ref[...] = matmul(a_s[...], wq_s[...]).astype(LOW)
        lane = lax.broadcasted_iota(jnp.int32, (tokens, 128), 1)
        lse_all = jnp.zeros((tokens, 128), F32)
        for h in range(heads):
            at = 3 * HS * h
            q = qkv_ref[:, at : at + HS]
            k = qkv_ref[:, at + HS : at + 2 * HS]
            v = qkv_ref[:, at + 2 * HS : at + 3 * HS]
            scores = matmul_t(q, k) * HS ** (-0.5)
            scores = jnp.where(mask_s[...] > 0, scores, NEG_FILL)
            top = jnp.max(scores, axis=1, keepdims=True)
            weights = jnp.exp(scores - top)
            total = jnp.sum(weights, axis=1, keepdims=True)
            lse_all = jnp.where(lane == h, top + jnp.log(total), lse_all)
            probs = (weights / total).astype(LOW)
            att_ref[:, h * HS : (h + 1) * HS] = matmul(probs, v).astype(LOW)
        lse_ref[...] = lse_all

    outs = [
        shape((tokens, wide), LOW),
        shape((tokens, 128), F32),
        shape((tokens, heads * HS), LOW),
    ]
    scratch = [
        pltpu.VMEM((tokens, width), LOW),
        pltpu.VMEM((width, wide), LOW),
        pltpu.VMEM((tokens, tokens), F32),
    ]
    flops = 2 * tokens * width * wide + 4 * heads * tokens * tokens * HS
    return run(body, outs, (*acts, *weights), (spots,), scratch, flops, spare=16)


def product_out(left, weights, start, count):
    groups = len(weights)
    tokens, wide = left.shape
    part = weights[0].shape[0] - start
    width = part * groups

    def body(*refs):
        weights, refs = refs[:groups], refs[groups:]
        left_ref, own_ref, other_ref, all_s, sem = refs
        wait(stage(stacked([w.at[pl.ds(start, part)] for w in weights], all_s), sem))
        halves_out(lambda o, n: left_ref[o : o + n, :], all_s[...], own_ref, other_ref)

    outs = [
        shape((tokens // 2, width), F32),
        shape((count, tokens // 2 // count, width), LOW),
    ]
    scratch = [pltpu.VMEM((width, wide), LOW)]
    flops = 2 * tokens * width * wide
    return run(body, outs, weights, (left,), scratch, flops)


def attention_backward(acts, wq, wo, qkv, lse, spots):
    count, groups = len(acts), len(wq)
    rows, width = acts[0].shape
    tokens, wide = rows * count, qkv.shape[1]
    heads = wide // (3 * HS)

    def body(*refs):
        acts, refs = refs[:count], refs[count:]
        wq, refs = refs[:groups], refs[groups:]
        wo, refs = refs[:groups], refs[groups:]
        qkv_ref, lse_ref, row_ref, grad_ref, own_ref, other_ref = refs[:6]
        a_s, wq_s, wo_s, mask_s, in_s, sem = refs[6:]
        jobs = stacked(acts, a_s)
        copies = stage(jobs + stacked(wo, wo_s) + stacked(wq, wq_s), sem)
        spots = row_ref[...]
        turned = spots.T
        mask_s[...] = (
            (spots[0:1, :] <= turned[:, 0:1]) & (spots[1:2, :] == turned[:, 1:2])
        ).astype(F32)
        wait(copies[: count + groups])
        in_s[...] = matmul(a_s[...], wo_s[...]).astype(LOW)
        for h in range(heads):
            at = 3 * HS * h
            q = qkv_ref[:, at : at + HS]
            k = qkv_ref[:, at + HS : at + 2 * HS]
            v = qkv_ref[:, at + 2 * HS : at + 3 * HS]
            up = in_s[:, h * HS : (h + 1) * HS]
            scores = matmul_t(q, k) * HS ** (-0.5)
            scores = jnp.where(mask_s[...] > 0, scores, NEG_FILL)
            probs = jnp.exp(scores - lse_ref[:, h : h + 1])
            dprobs = matmul_t(up, v)
            delta = jnp.sum(probs * dprobs, axis=1, keepdims=True)
            dscores = (probs * (dprobs - delta)).astype(LOW)
            grad_ref[:, at : at + HS] = (matmul(dscores, k) * HS ** (-0.5)).astype(LOW)
            grad_ref[:, at + HS : at + 2 * HS] = (
                t_matmul(dscores, q) * HS ** (-0.5)
            ).astype(LOW)
            grad_ref[:, at + 2 * HS : at + 3 * HS] = t_matmul(probs.astype(LOW), up).astype(LOW)
        wait(copies[count + groups :])
        halves_out(lambda o, n: grad_ref[o : o + n, :], wq_s[...], own_ref, other_ref)

    outs = [
        shape((tokens, wide), LOW),
        shape((tokens // 2, width), F32),
        shape((count // 2, rows, width), LOW),
    ]
    scratch = [
        pltpu.VMEM((tokens, width), LOW),
        pltpu.VMEM((width, wide), LOW),
        pltpu.VMEM((width, heads * HS), LOW),
        pltpu.VMEM((tokens, tokens), F32),
        pltpu.VMEM((tokens, heads * HS), LOW),
    ]
    flops = 2 * tokens * width * (wide + heads * HS) + 10 * heads * tokens * tokens * HS
    return run(body, outs, (*acts, *wq, *wo), (qkv, lse, spots), scratch, flops, spare=16)


CURVE = (2.0 / 3.141592653589793) ** 0.5
CUBE = 0.044715


def two_weights(pieces, up_s, down_s):
    rows = pieces[0].shape[0] // 2
    jobs = []
    for i, piece in enumerate(pieces):
        jobs.append((piece.at[pl.ds(0, rows)], up_s.at[pl.ds(i * rows, rows)]))
        jobs.append((piece.at[pl.ds(rows, rows)], down_s.at[pl.ds(i * rows, rows)]))
    return jobs


def mlp_middle(acts, outer, weights):
    count, groups = len(acts), len(weights)
    rows, width = acts[0].shape
    tokens, wide = rows * count, weights[0].shape[1]

    def body(*refs):
        acts, refs = refs[:count], refs[count:]
        outer, refs = refs[:count], refs[count:]
        weights, refs = refs[:groups], refs[groups:]
        hidden_ref, grad_ref, own_ref, other_ref, a_s, o_s, up_s, down_s, sem = refs
        jobs = stacked(acts, a_s) + stacked(outer, o_s) + two_weights(weights, up_s, down_s)
        wait(stage(jobs, sem))
        for at in (slice(0, tokens // 2), slice(tokens // 2, tokens)):
            pre = matmul(a_s[at, :], up_s[...])
            upper = matmul(o_s[at, :], down_s[...])
            square = pre * pre
            bent = jnp.tanh(CURVE * (pre + CUBE * square * pre))
            hidden_ref[at, :] = (0.5 * pre * (1.0 + bent)).astype(LOW)
            rate = 0.5 * (1.0 + bent) + 0.5 * pre * (1.0 - bent * bent) * (
                CURVE * (1.0 + 3.0 * CUBE * square)
            )
            grad_ref[at, :] = (rate * upper).astype(LOW)
        halves_out(lambda o, n: grad_ref[o : o + n, :], up_s[...], own_ref, other_ref)

    outs = [
        shape((tokens, wide), LOW),
        shape((tokens, wide), LOW),
        shape((tokens // 2, width), F32),
        shape((count // 2, rows, width), LOW),
    ]
    scratch = [
        pltpu.VMEM((tokens, width), LOW),
        pltpu.VMEM((tokens, width), LOW),
        pltpu.VMEM((width, wide), LOW),
        pltpu.VMEM((width, wide), LOW),
    ]
    flops = 6 * tokens * width * wide
    return run(body, outs, (*acts, *outer, *weights), (), scratch, flops)


def weight_grads(first, first_grad, second, second_grad, groups, beside):
    count = len(first)
    rows, width = first[0].shape
    tokens, part = rows * count, width // groups
    wide, wide2 = first_grad.shape[1], second_grad.shape[1]
    spot = (0, wide) if beside else (part, 0)
    dims = (part, wide + wide2) if beside else (2 * part, wide)

    def body(*refs):
        first, refs = refs[:count], refs[count:]
        second, refs = refs[:count], refs[count:]
        grad_ref, grad2_ref, own_ref, *rest, a_s, b_s, prod_s, prod2_s, sem = refs
        copies = stage(stacked(first, a_s) + stacked(second, b_s), sem)
        wait(copies[:count])
        prod_s[...] = t_matmul(a_s[...], grad_ref[...])
        wait(copies[count:])
        prod2_s[...] = t_matmul(b_s[...], grad2_ref[...])
        for k, ref in enumerate((own_ref, *rest)):
            one = prod_s[k * part : (k + 1) * part, :].astype(ref.dtype)
            two = prod2_s[k * part : (k + 1) * part, :].astype(ref.dtype)
            ref[0:part, 0:wide] = one
            ref[spot[0] : spot[0] + part, spot[1] : spot[1] + wide2] = two

    outs = [shape(dims, F32)] + [shape(dims, LOW)] * (groups - 1)
    scratch = [
        pltpu.VMEM((tokens, width), LOW),
        pltpu.VMEM((tokens, width), LOW),
        pltpu.VMEM((width, wide), F32),
        pltpu.VMEM((width, wide2), F32),
    ]
    flops = 2 * tokens * width * (wide + wide2)
    return run(body, outs, (*first, *second), (first_grad, second_grad), scratch, flops)


def step_rule(param, grad, first, second, decay):
    first = BETA_ONE * first + (1.0 - BETA_ONE) * grad
    second = BETA_TWO * second + (1.0 - BETA_TWO) * grad * grad
    first_hat = first / (1.0 - BETA_ONE**STEP_COUNT)
    second_hat = second / (1.0 - BETA_TWO**STEP_COUNT)
    updated = param - RATE * (first_hat / (jnp.sqrt(second_hat) + ADAM_EPS) + decay * param)
    return updated, first, second


def adamw(param, grad, state, decay):
    updated, first, second = step_rule(param, grad, state[0], state[1], decay)
    return updated, jnp.stack([first, second])


def update_two(parts, param, state, param2, state2, beside):
    part, wide = param.shape
    wide2 = param2.shape[1]
    count = len(parts)
    spot = (0, wide) if beside else (part, 0)

    def body(*refs):
        parts, refs = refs[:count], refs[count:]
        ins, outs = refs[:4], refs[4:10]
        for i, (row, col, size) in enumerate(((0, 0, wide), (*spot, wide2))):
            param_ref, state_ref = ins[2 * i : 2 * i + 2]
            grad_ref, new_ref, next_ref = outs[3 * i : 3 * i + 3]
            grad = sum(
                [p[row : row + part, col : col + size].astype(F32) for p in parts[1:]],
                parts[0][row : row + part, col : col + size],
            )
            grad_ref[...] = grad
            new_ref[...], next_ref[0], next_ref[1] = step_rule(
                param_ref[...], grad, state_ref[0], state_ref[1], DECAY
            )

    outs = []
    for size in (wide, wide2):
        outs += [shape((part, size), F32)] * 2 + [shape((2, part, size), F32)]
    return run(body, outs, (), (*parts, param, state, param2, state2))


def shards(
    nrow,
    ncol,
    layer_input,
    output_grad,
    w_qkv,
    w_out,
    w_up,
    w_down,
    layernorm_params,
    state_qkv,
    state_out,
    state_up,
    state_down,
    state_norms,
    segment_ids,
):
    grid = Grid(nrow, ncol)
    own_tokens = layer_input.shape[0] // nrow
    row_tokens = own_tokens * ncol

    def flip(x):
        return jnp.swapaxes(x, -1, -2)

    x_t, grad_t = flip(layer_input), flip(output_grad)
    shift = (grid.lin % nrow) ^ grid.row
    pieces = grid.to_tokens(entry(grid.row, x_t, grad_t, layernorm_params, nrow))
    hat1, inverse1, a1_own, x, out_low, params = norm_first(shift, pieces, own_tokens)

    block = w_qkv.shape[0]

    def tidy(pieces):
        if block % 16 == 0:
            return pieces
        parts = range(0, pieces[0].shape[0], block)
        return [jnp.concatenate([p[at : at + block] for at in parts for p in pieces])]

    wq = tidy(grid.gather_row(w_qkv.astype(LOW)))
    wo = tidy(grid.gather_row(w_out.T.astype(LOW)))
    w_mlp_own = jnp.concatenate([w_up.astype(LOW), w_down.T.astype(LOW)])
    w_mlp = tidy(grid.gather_row(w_mlp_own))

    chip, core = grid.col // 2, grid.col % 2
    spot = jnp.arange(row_tokens)
    sequence = spot // segment_ids.shape[1]
    marks = sequence * (1 + jnp.max(segment_ids)) + segment_ids.reshape(-1)

    def reorder(values):
        values = values.reshape(grid.nz, 2, own_tokens)
        chips = select_xor([values[z] for z in range(grid.nz)], chip)
        cores = select_xor([jnp.stack([v[h] for v in chips]) for h in range(2)], core)
        return jnp.concatenate(cores).reshape(-1)

    order = jnp.stack([reorder(spot), reorder(marks)]).astype(F32)
    spots = jnp.pad(order, ((0, 6), (0, 0)))

    a1 = grid.gather_col(after(a1_own, spots, w_mlp_own))
    out_full = grid.gather_col(after(out_low, a1[: grid.nz]))
    qkv, lse, attended = attention_forward(a1, wq, spots)
    partial_sums = product_out(attended, wo, 0, grid.nz)
    parts = grid.reduce_col(*partial_sums)
    hat2, inverse2, a2_own, attn_sum = norm_second(parts, x, params)
    a2 = grid.gather_col(a2_own)
    hidden, pre_grad, *partial_sums = mlp_middle(a2, out_full, w_mlp)
    parts = grid.reduce_col(*partial_sums)
    mine, *rest = weight_grads(a2, after(pre_grad, parts[0]), out_full, hidden, nrow, beside=False)
    mlp_parts = [mine] + grid.send_row(rest)
    middle_low_own, back2, terms2 = norm_second_back(
        parts, hat2, inverse2, params, out_low
    )
    middle_low = grid.gather_col(middle_low_own)
    own, other = product_out(after(hidden, middle_low_own), w_mlp, w_mlp[0].shape[0] // 2, grid.nz)
    out_parts = [attn_sum] + grid.reduce_col(own, other)
    qkv_grad, *partial_sums = attention_backward(
        middle_low, wq, wo, qkv, lse, spots
    )
    parts = grid.reduce_col(*partial_sums)
    mine, *rest = weight_grads(
        a1, after(qkv_grad, parts[0]), middle_low, attended, nrow, beside=True
    )
    attn_parts = [mine] + grid.send_row(rest)
    *pieces, terms = norm_first_back(
        shift, parts, hat1, inverse1, params, back2, terms2, out_parts, nrow
    )
    pieces = grid.to_widths(pieces)
    results = leave(grid.row, pieces, x_t, grad_t)
    layer_input_grad, block_output = map(flip, results)
    terms = sum(grid.send_row([terms[k] for k in range(1, nrow)]), terms[0])
    terms = terms + grid.over_core(terms)
    norm_params_grad = sum(grid.send_chips([terms] * (grid.nz - 1)), terms)

    grad_up, new_up, next_state_up, *rest = update_two(
        mlp_parts, w_up, state_up, flip(w_down), flip(state_down), beside=False
    )
    grad_down, new_down, next_state_down = map(flip, rest)
    grad_qkv, new_qkv, next_state_qkv, *rest = update_two(
        attn_parts, w_qkv, state_qkv, flip(w_out), flip(state_out), beside=True
    )
    grad_out, new_out, next_state_out = map(flip, rest)
    new_norms, next_state_norms = adamw(layernorm_params, norm_params_grad, state_norms, 0.0)
    return (
        block_output,
        layer_input_grad,
        grad_qkv,
        grad_out,
        grad_up,
        grad_down,
        norm_params_grad,
        new_qkv,
        new_out,
        new_up,
        new_down,
        new_norms,
        next_state_qkv,
        next_state_out,
        next_state_up,
        next_state_down,
        next_state_norms,
    )


def solution(mesh):
    tokens = P("col", "row")
    wide, tall = P("row", "col"), P("col", "row")

    def body(*args):
        return shards(mesh.shape["row"], mesh.shape["col"], *args)

    return jax.shard_map(
        body,
        mesh=mesh,
        in_specs=(
            tokens,
            tokens,
            wide,
            tall,
            wide,
            tall,
            P(None, "row"),
            P(None, "row", "col"),
            P(None, "col", "row"),
            P(None, "row", "col"),
            P(None, "col", "row"),
            P(None, None, "row"),
            P("row", None),
        ),
        out_specs=(
            tokens,
            tokens,
            wide,
            tall,
            wide,
            tall,
            P(None, "row"),
            wide,
            tall,
            wide,
            tall,
            P(None, "row"),
            P(None, "row", "col"),
            P(None, "col", "row"),
            P(None, "row", "col"),
            P(None, "col", "row"),
            P(None, None, "row"),
        ),
        check_vma=False,
    )
```
